32 devices in a mesh: section: 2 (over y), dp: 16 (over z, x, core).
Axes of the slice: x: 2, y: 2, z: 4, core: 2. Of those that a mesh axis runs over, the one named last changes fastest.
Arguments:
- inputs: bfloat16 [2, 16, 64, 1024], P(None, 'dp'), may hold values from -6 to 6
- cotangent: bfloat16 [2, 16, 64, 1024], P(None, 'dp'), may hold values from -6 to 6
- live_slots: int32 [2, 16], P(None, 'dp'), may hold values 0 or 1
- norm1_gain: bfloat16 [2, 1024], P('section', 'dp'), may hold values from 0.099609375 to 1.8984375
- norm1_bias: bfloat16 [2, 1024], P('section', 'dp'), may hold values from -4 to 4
- qkv_weight: bfloat16 [2, 1024, 3072], P('section', 'dp')
- qv_bias: bfloat16 [2, 2048], P('section', 'dp'), may hold values from -6 to 6
- out_weight: bfloat16 [2, 1024, 1024], P('section', 'dp'), may hold values from -0.75 to 0.75
- out_bias: bfloat16 [2, 1024], P('section', 'dp'), may hold values from -4 to 4
- norm2_gain: bfloat16 [2, 1024], P('section', 'dp'), may hold values from 0.099609375 to 1.8984375
- norm2_bias: bfloat16 [2, 1024], P('section', 'dp'), may hold values from -4 to 4
- fc1_weight: bfloat16 [2, 1024, 4096], P('section', 'dp'), may hold values from -0.1875 to 0.1875
- fc1_bias: bfloat16 [2, 4096], P('section', 'dp'), may hold values from -6 to 6
- fc2_weight: bfloat16 [2, 4096, 1024], P('section', 'dp'), may hold values from -0.09375 to 0.09375
- fc2_bias: bfloat16 [2, 1024], P('section', 'dp'), may hold values from -4 to 4
Outputs:
- outputs: bfloat16 [2, 2, 16, 64, 1024], P('section', None, 'dp')
- in_grads: float32 [2, 2, 16, 64, 1024], P('section', None, 'dp')
- norm1_gain_grad: float32 [2, 1024], P('section', 'dp')
- norm1_bias_grad: float32 [2, 1024], P('section', 'dp')
- qkv_weight_grad: float32 [2, 1024, 3072], P('section', 'dp')
- qv_bias_grad: float32 [2, 2048], P('section', 'dp')
- out_weight_grad: float32 [2, 1024, 1024], P('section', 'dp')
- out_bias_grad: float32 [2, 1024], P('section', 'dp')
- norm2_gain_grad: float32 [2, 1024], P('section', 'dp')
- norm2_bias_grad: float32 [2, 1024], P('section', 'dp')
- fc1_weight_grad: float32 [2, 1024, 4096], P('section', 'dp')
- fc1_bias_grad: float32 [2, 4096], P('section', 'dp')
- fc2_weight_grad: float32 [2, 4096, 1024], P('section', 'dp')
- fc2_bias_grad: float32 [2, 1024], P('section', 'dp')
The draws below stay inside these ranges and needn't reach their ends.
All inputs are finite; a program needn't handle non-finite values. No bound on the sum of `live_slots` on one device may be relied on, other than what follows from the above.
Results may differ from the reference program's by a relative error of at most 0.018.
Values may be sent and summed in bfloat16 or wider, within the bound.
A program may use at most 192 MiB of HBM per device.

```python
import jax
import jax.numpy as jnp
from jax import lax

D = 1024
HEAD_DIM = 64
FF = 4096
SEQ = 64
MB = 2
IMAGES = 16
N_SECTION = 2


def draw_qkv_weight(key, part):
    key_base = jax.random.fold_in(key, 0)
    base_draw = jax.random.normal(key_base, (N_SECTION, D, 3 * D), jnp.float32) * D ** (-0.5)
    return base_draw.astype(jnp.bfloat16)


def place_ends(drawn, stream_key, least, top_value):
    index_at = [jax.random.randint(jax.random.fold_in(stream_key, axis), (), 0, length) for axis, length in enumerate(drawn.shape)]
    main_axis = drawn.shape.index(max(drawn.shape))
    next_to = index_at[:main_axis] + [(index_at[main_axis] + 1) % drawn.shape[main_axis]] + index_at[main_axis + 1:]
    return drawn.at[tuple(index_at)].set(least).at[tuple(next_to)].set(top_value)


def strengthened(values, key, source, target, parts, factor):
    owner, partner = [(jnp.arange(values.shape[axis_at]) // (values.shape[axis_at] // parts)).reshape([-1 if axis == axis_at else 1 for axis in range(values.ndim)]) for axis_at in (source, target)]
    chosen = jax.random.permutation(key, parts)[partner]
    strong = (owner == chosen) | (owner == (partner + parts // 2) % parts)
    return jnp.where(strong, factor * values, values)


def shard_levels(stream_key, dims, cuts, least, top_value):
    loudness, own = 1.0, jax.random.fold_in(stream_key, 6)
    for dim, shards_of in cuts:
        draws = jnp.exp(jax.random.uniform(jax.random.fold_in(own, dim), (shards_of,), jnp.float32, least / len(cuts), top_value / len(cuts)))
        loudness = loudness * jnp.repeat(draws, dims[dim] // shards_of).reshape([-1 if axis == dim else 1 for axis in range(len(dims))])
    return loudness


def normal_values(rng, extent, scale, most, cuts=(), held_as=jnp.bfloat16):
    values = scale * jax.random.normal(rng, extent, jnp.float32)
    if cuts:
        values = values * shard_levels(rng, extent, cuts, -0.22, 0.18)
    return jnp.clip(values, -most, most).astype(held_as)


def heavy_noise(own_key, extent, scale, bound, shards, heavy, held_as=jnp.bfloat16):
    values = scale * jax.random.normal(own_key, extent, jnp.float32)
    if shards:
        values = values * shard_levels(own_key, extent, shards, -0.22, 0.18)
    return jnp.clip(strengthened(values, jax.random.fold_in(own_key, 3), *heavy), -bound, bound).astype(held_as)


def setup_inputs(seed: int = 0) -> dict:
    streams_of = jax.random.split(jax.random.key(seed), 16)
    return {
        "inputs": heavy_noise(streams_of[0], (MB, IMAGES, SEQ, D), 1.0, 6.0, ((1, 16),), (1, 3, 16, 2.0)),
        "cotangent": heavy_noise(streams_of[1], (MB, IMAGES, SEQ, D), 1.0, 6.0, ((1, 16),), (1, 3, 16, 2.0)),
        "live_slots": place_ends((jax.random.randint(streams_of[2], (MB, IMAGES), 0, 4) < 3).astype(jnp.int32), jax.random.fold_in(streams_of[2], 1), 0, 1),
        "norm1_gain": jnp.clip(1.0 + 0.18 * jax.random.normal(streams_of[3], (N_SECTION, D), jnp.float32), 0.099609375, 1.8984375).astype(jnp.bfloat16),
        "norm1_bias": normal_values(streams_of[4], (N_SECTION, D), 0.3, 4.0, ((0, 2), (1, 16))),
        "qkv_weight": draw_qkv_weight(jax.random.fold_in(streams_of[15], 71), 0),
        "qv_bias": normal_values(streams_of[6], (N_SECTION, 2 * D), 0.5, 6.0, ((0, 2), (1, 16))),
        "out_weight": normal_values(streams_of[7], (N_SECTION, D, D), (D // 16) ** -0.5, 0.75, ((0, 2), (1, 16))),
        "out_bias": normal_values(streams_of[8], (N_SECTION, D), 0.3, 4.0, ((0, 2), (1, 16))),
        "norm2_gain": jnp.clip(1.0 + 0.18 * jax.random.normal(streams_of[9], (N_SECTION, D), jnp.float32), 0.099609375, 1.8984375).astype(jnp.bfloat16),
        "norm2_bias": normal_values(streams_of[10], (N_SECTION, D), 0.3, 4.0, ((0, 2), (1, 16))),
        "fc1_weight": normal_values(streams_of[11], (N_SECTION, D, FF), D ** -0.5, 0.1875, ((0, 2), (1, 16))),
        "fc1_bias": normal_values(streams_of[12], (N_SECTION, FF), 0.5, 6.0, ((0, 2), (1, 16))),
        "fc2_weight": normal_values(streams_of[13], (N_SECTION, FF, D), FF ** -0.5, 0.09375, ((0, 2), (1, 16))),
        "fc2_bias": normal_values(streams_of[14], (N_SECTION, D), 0.3, 4.0, ((0, 2), (1, 16))),
    }


EPSILON = 1e-06
ROOT_HALF = 0.7071067811865476
INV_ROOT_TWO_PI = 0.3989422804014327

def norm_parts(stream):
    average = lax.optimization_barrier(jnp.mean(stream, axis=-1, keepdims=True))
    centred = stream - average
    inv_std = lax.rsqrt(lax.optimization_barrier(jnp.mean(centred * centred, axis=-1, keepdims=True)) + EPSILON)
    return (centred * inv_std, inv_std)

def norm_back(signal, normed, inv_std):
    first_mean = lax.optimization_barrier(jnp.mean(signal, axis=-1, keepdims=True))
    second_mean = lax.optimization_barrier(jnp.mean(signal * normed, axis=-1, keepdims=True))
    return inv_std * (signal - first_mean - normed * second_mean)

def gelu_value(pre_act):
    return 0.5 * pre_act * (1.0 + lax.erf(pre_act * ROOT_HALF))

def gelu_slope(pre_act):
    return 0.5 * (1.0 + lax.erf(pre_act * ROOT_HALF)) + pre_act * jnp.exp(-0.5 * pre_act * pre_act) * INV_ROOT_TWO_PI

def layer_forward(stream, live_scale, params):
    norm1_gain, norm1_bias, qkv_weight, qv_bias, out_weight, out_bias, norm2_gain, norm2_bias, fc1_weight, fc1_bias, fc2_weight, fc2_bias = params
    images, length, model_width = stream.shape
    heads_shape = (images, length, model_width // HEAD_DIM, HEAD_DIM)
    scaling = HEAD_DIM ** (-0.5)
    wide_in = stream.astype(jnp.float32)
    normal_one, inv_one = norm_parts(wide_in)
    normed1 = (normal_one * norm1_gain + norm1_bias).astype(jnp.bfloat16)
    projected = jnp.dot(normed1, qkv_weight, preferred_element_type=jnp.float32)
    query_rows = (projected[..., :model_width] + qv_bias[:model_width]).astype(jnp.bfloat16)
    key_rows = projected[..., model_width:2 * model_width].astype(jnp.bfloat16)
    value_rows = (projected[..., 2 * model_width:] + qv_bias[model_width:]).astype(jnp.bfloat16)
    scores = jnp.einsum('bqhe,bkhe->bhqk', query_rows.reshape(heads_shape).astype(jnp.float32), key_rows.reshape(heads_shape).astype(jnp.float32)) * scaling
    top_score = lax.optimization_barrier(jnp.max(scores, axis=-1, keepdims=True))
    exp_scores = jnp.exp(scores - top_score)
    totals = lax.optimization_barrier(jnp.sum(exp_scores, axis=-1, keepdims=True))
    log_total = top_score + jnp.log(totals)
    attn_probs = (exp_scores / totals).astype(jnp.bfloat16)
    context = jnp.einsum('bhqk,bkhe->bqhe', attn_probs.astype(jnp.float32), value_rows.reshape(heads_shape).astype(jnp.float32))
    context = context.reshape(images, length, model_width).astype(jnp.bfloat16)
    middle = wide_in + jnp.dot(context, out_weight, preferred_element_type=jnp.float32) + out_bias
    normal_two, inv_two = norm_parts(middle)
    normed2 = (normal_two * norm2_gain + norm2_bias).astype(jnp.bfloat16)
    pre_act = jnp.dot(normed2, fc1_weight, preferred_element_type=jnp.float32) + fc1_bias
    activated = gelu_value(pre_act).astype(jnp.bfloat16)
    result = live_scale * (middle + jnp.dot(activated, fc2_weight, preferred_element_type=jnp.float32) + fc2_bias)
    saved_inputs = (stream, query_rows, key_rows, value_rows, log_total, context, middle, pre_act, activated)
    return (result.astype(jnp.bfloat16), saved_inputs)

def outer_rows(left_rows, right_rows):
    return jnp.dot(left_rows.reshape(-1, left_rows.shape[-1]).T, right_rows.reshape(-1, right_rows.shape[-1]), preferred_element_type=jnp.float32)

def layer_backward(grad_out, live_scale, saved_inputs, params):
    norm1_gain, norm1_bias, qkv_weight, qv_bias, out_weight, out_bias, norm2_gain, norm2_bias, fc1_weight, fc1_bias, fc2_weight, fc2_bias = params
    stream, query_rows, key_rows, value_rows, log_total, context, middle, pre_act, activated = saved_inputs
    images, length, model_width = stream.shape
    heads_shape = (images, length, model_width // HEAD_DIM, HEAD_DIM)
    scaling = HEAD_DIM ** (-0.5)
    masked = live_scale * grad_out
    masked_half = masked.astype(jnp.bfloat16)
    grad_pre = jnp.dot(masked_half, fc2_weight.T, preferred_element_type=jnp.float32) * gelu_slope(pre_act)
    grad_pre_half = grad_pre.astype(jnp.bfloat16)
    grad_normed2 = jnp.dot(grad_pre_half, fc1_weight.T, preferred_element_type=jnp.float32)
    normal_two, inv_two = norm_parts(middle)
    grad_middle = masked + norm_back(grad_normed2 * norm2_gain, normal_two, inv_two)
    grad_middle_half = grad_middle.astype(jnp.bfloat16)
    grad_context = jnp.dot(grad_middle_half, out_weight.T, preferred_element_type=jnp.float32).astype(jnp.bfloat16)
    query_heads = query_rows.reshape(heads_shape).astype(jnp.float32)
    key_heads = key_rows.reshape(heads_shape).astype(jnp.float32)
    value_heads = value_rows.reshape(heads_shape).astype(jnp.float32)
    context_heads = grad_context.reshape(heads_shape).astype(jnp.float32)
    scores = jnp.einsum('bqhe,bkhe->bhqk', query_heads, key_heads) * scaling
    probs_wide = jnp.exp(scores - log_total)
    probs_half = probs_wide.astype(jnp.bfloat16)
    grad_probs = jnp.einsum('bqhe,bkhe->bhqk', context_heads, value_heads)
    row_delta = lax.optimization_barrier(jnp.sum(probs_wide * grad_probs, axis=-1, keepdims=True))
    grad_scores = (probs_wide * (grad_probs - row_delta) * scaling).astype(jnp.bfloat16).astype(jnp.float32)
    grad_query = jnp.einsum('bhqk,bkhe->bqhe', grad_scores, key_heads).reshape(images, length, model_width)
    grad_keys = jnp.einsum('bhqk,bqhe->bkhe', grad_scores, query_heads).reshape(images, length, model_width)
    grad_values = jnp.einsum('bhqk,bqhe->bkhe', probs_half.astype(jnp.float32), context_heads).reshape(images, length, model_width)
    grad_proj = jnp.concatenate([grad_query, grad_keys, grad_values], axis=-1).astype(jnp.bfloat16)
    grad_normed1 = jnp.dot(grad_proj, qkv_weight.T, preferred_element_type=jnp.float32)
    wide_in = stream.astype(jnp.float32)
    normal_one, inv_one = norm_parts(wide_in)
    normed1 = (normal_one * norm1_gain + norm1_bias).astype(jnp.bfloat16)
    normed2 = (normal_two * norm2_gain + norm2_bias).astype(jnp.bfloat16)
    grad_stream = grad_middle + norm_back(grad_normed1 * norm1_gain, normal_one, inv_one)
    both_axes = (0, 1)
    grads = (lax.optimization_barrier(jnp.sum(grad_normed1 * normal_one, axis=both_axes)), lax.optimization_barrier(jnp.sum(grad_normed1, axis=both_axes)), outer_rows(normed1, grad_proj), jnp.concatenate([lax.optimization_barrier(jnp.sum(grad_query, axis=both_axes)), lax.optimization_barrier(jnp.sum(grad_values, axis=both_axes))]), outer_rows(context, grad_middle_half), lax.optimization_barrier(jnp.sum(grad_middle, axis=both_axes)), lax.optimization_barrier(jnp.sum(grad_normed2 * normal_two, axis=both_axes)), lax.optimization_barrier(jnp.sum(grad_normed2, axis=both_axes)), outer_rows(normed2, grad_pre_half), lax.optimization_barrier(jnp.sum(grad_pre, axis=both_axes)), outer_rows(activated, masked_half), lax.optimization_barrier(jnp.sum(masked, axis=both_axes)))
    return (grad_stream, grads)

def reference(inputs, cotangent, live_slots, norm1_gain, norm1_bias, qkv_weight, qv_bias, out_weight, out_bias, norm2_gain, norm2_bias, fc1_weight, fc1_bias, fc2_weight, fc2_bias):
    everything = (norm1_gain, norm1_bias, qkv_weight, qv_bias, out_weight, out_bias, norm2_gain, norm2_bias, fc1_weight, fc1_bias, fc2_weight, fc2_bias)
    first_params = tuple((member[0] for member in everything))
    second_params = tuple((member[1] for member in everything))
    first_accum = [jnp.zeros(member.shape[1:], jnp.float32) for member in everything]
    second_accum = [jnp.zeros(member.shape[1:], jnp.float32) for member in everything]
    first_outs, second_outs, first_backs, second_backs = ([], [], [], [])
    for microbatch_index in range(MB):
        live_scale = live_slots[microbatch_index].astype(jnp.float32)[:, None, None]
        first_out, first_stash = layer_forward(inputs[microbatch_index], live_scale, first_params)
        second_out, second_stash = layer_forward(first_out, live_scale, second_params)
        second_back, second_grads = layer_backward(cotangent[microbatch_index].astype(jnp.float32), live_scale, second_stash, second_params)
        first_back, first_grads = layer_backward(second_back, live_scale, first_stash, first_params)
        first_accum = [accum + grad_part for accum, grad_part in zip(first_accum, first_grads)]
        second_accum = [accum + grad_part for accum, grad_part in zip(second_accum, second_grads)]
        first_outs.append(first_out)
        second_outs.append(second_out)
        first_backs.append(first_back)
        second_backs.append(second_back)
    outputs = jnp.stack([jnp.stack(first_outs), jnp.stack(second_outs)])
    in_grads = jnp.stack([jnp.stack(first_backs), jnp.stack(second_backs)])
    stacked = [jnp.stack([first_part, second_part]) for first_part, second_part in zip(first_accum, second_accum)]
    return (outputs, in_grads, stacked[0], stacked[1], stacked[2], stacked[3], stacked[4], stacked[5], stacked[6], stacked[7], stacked[8], stacked[9], stacked[10], stacked[11])
```

```python
import jax
import jax.numpy as jnp
from jax import lax
from jax.sharding import PartitionSpec as P

HEAD_DIM = 64
LANES = 128


EPSILON = 1e-06
ROOT_HALF = 0.7071067811865476
INV_ROOT_TWO_PI = 0.3989422804014327


def passed_along(value, axis, steps):
    count = lax.axis_size(axis)
    leading, last = (max(0, -steps), min(count, count - steps))
    return lax.ppermute(value, axis, [(source, source + steps) for source in range(leading, last)])


def norm_parts(stream):
    average = jnp.mean(stream, axis=-1, keepdims=True)
    centred = stream - average
    inv_std = lax.rsqrt(jnp.mean(centred * centred, axis=-1, keepdims=True) + EPSILON)
    return (centred * inv_std, inv_std)


def norm_back(signal, normed, inv_std):
    first_mean = jnp.mean(signal, axis=-1, keepdims=True)
    second_mean = jnp.mean(signal * normed, axis=-1, keepdims=True)
    return inv_std * (signal - first_mean - normed * second_mean)


def gelu_value(pre_act):
    return 0.5 * pre_act * (1.0 + lax.erf(pre_act * ROOT_HALF))


def gelu_slope(pre_act):
    return (
        0.5 * (1.0 + lax.erf(pre_act * ROOT_HALF))
        + pre_act * jnp.exp(-0.5 * pre_act * pre_act) * INV_ROOT_TWO_PI
    )


def matmul(left_rows, weight):
    return jnp.einsum("bsd,de->bse", left_rows, weight, preferred_element_type=jnp.float32)


def transposed_product(left_rows, weight):
    return jnp.einsum("bse,de->bsd", left_rows, weight, preferred_element_type=jnp.float32)


def layer_forward(stream, live_scale, params):
    (
        norm1_gain,
        norm1_bias,
        qkv_weight,
        qv_bias,
        out_weight,
        out_bias,
        norm2_gain,
        norm2_bias,
        fc1_weight,
        fc1_bias,
        fc2_weight,
        fc2_bias,
    ) = params
    images, length, model_width = stream.shape
    heads_shape = (images, length, model_width // HEAD_DIM, HEAD_DIM)
    scaling = HEAD_DIM ** (-0.5)
    wide_in = stream.astype(jnp.float32)
    normal_one, inv_one = norm_parts(wide_in)
    normed1 = (normal_one * norm1_gain + norm1_bias).astype(jnp.bfloat16)
    projected = matmul(normed1, qkv_weight)
    query_rows = (projected[..., :model_width] + qv_bias[:model_width]).astype(jnp.bfloat16)
    key_rows = projected[..., model_width : 2 * model_width].astype(jnp.bfloat16)
    value_rows = (projected[..., 2 * model_width :] + qv_bias[model_width:]).astype(jnp.bfloat16)
    scores = (
        jnp.einsum(
            "bqhe,bkhe->bhqk",
            query_rows.reshape(heads_shape),
            key_rows.reshape(heads_shape),
            preferred_element_type=jnp.float32,
        )
        * scaling
    )
    top_score = jnp.max(scores, axis=-1, keepdims=True)
    exp_scores = jnp.exp(scores - top_score)
    totals = jnp.sum(exp_scores, axis=-1, keepdims=True)
    log_total = top_score + jnp.log(totals)
    attn_probs = (exp_scores / totals).astype(jnp.bfloat16)
    context = jnp.einsum(
        "bhqk,bkhe->bqhe",
        attn_probs,
        value_rows.reshape(heads_shape),
        preferred_element_type=jnp.float32,
    )
    context = context.reshape(images, length, model_width).astype(jnp.bfloat16)
    middle = wide_in + matmul(context, out_weight) + out_bias
    normal_two, inv_two = norm_parts(middle)
    normed2 = (normal_two * norm2_gain + norm2_bias).astype(jnp.bfloat16)
    pre_act = matmul(normed2, fc1_weight) + fc1_bias
    activated = gelu_value(pre_act).astype(jnp.bfloat16)
    result = live_scale * (middle + matmul(activated, fc2_weight) + fc2_bias)
    saved_inputs = (
        stream,
        query_rows,
        key_rows,
        value_rows,
        log_total,
        context,
        middle,
        pre_act,
        activated,
    )
    return (result.astype(jnp.bfloat16), saved_inputs)


def layer_backward(grad_out, live_scale, saved_inputs, params):
    (
        norm1_gain,
        norm1_bias,
        qkv_weight,
        qv_bias,
        out_weight,
        out_bias,
        norm2_gain,
        norm2_bias,
        fc1_weight,
        fc1_bias,
        fc2_weight,
        fc2_bias,
    ) = params
    stream, query_rows, key_rows, value_rows, log_total, context, middle, pre_act, activated = (
        saved_inputs
    )
    images, length, model_width = stream.shape
    heads_shape = (images, length, model_width // HEAD_DIM, HEAD_DIM)
    scaling = HEAD_DIM ** (-0.5)
    masked = live_scale * grad_out
    masked_half = masked.astype(jnp.bfloat16)
    grad_pre = transposed_product(masked_half, fc2_weight) * gelu_slope(pre_act)
    grad_pre_half = grad_pre.astype(jnp.bfloat16)
    grad_normed2 = transposed_product(grad_pre_half, fc1_weight)
    normal_two, inv_two = norm_parts(middle)
    grad_middle = masked + norm_back(grad_normed2 * norm2_gain, normal_two, inv_two)
    grad_middle_half = grad_middle.astype(jnp.bfloat16)
    grad_context = (
        transposed_product(grad_middle_half, out_weight).astype(jnp.bfloat16).reshape(heads_shape)
    )
    query_heads = query_rows.reshape(heads_shape)
    key_heads = key_rows.reshape(heads_shape)
    value_heads = value_rows.reshape(heads_shape)
    scores = (
        jnp.einsum("bqhe,bkhe->bhqk", query_heads, key_heads, preferred_element_type=jnp.float32)
        * scaling
    )
    probs_wide = jnp.exp(scores - log_total)
    probs_half = probs_wide.astype(jnp.bfloat16)
    grad_probs = jnp.einsum(
        "bqhe,bkhe->bhqk", grad_context, value_heads, preferred_element_type=jnp.float32
    )
    row_delta = jnp.sum(probs_wide * grad_probs, axis=-1, keepdims=True)
    grad_scores = (probs_wide * (grad_probs - row_delta) * scaling).astype(jnp.bfloat16)
    grad_query = jnp.einsum(
        "bhqk,bkhe->bqhe", grad_scores, key_heads, preferred_element_type=jnp.float32
    ).reshape(images, length, model_width)
    grad_keys = jnp.einsum(
        "bhqk,bqhe->bkhe", grad_scores, query_heads, preferred_element_type=jnp.float32
    ).reshape(images, length, model_width)
    grad_values = jnp.einsum(
        "bhqk,bqhe->bkhe", probs_half, grad_context, preferred_element_type=jnp.float32
    ).reshape(images, length, model_width)
    grad_proj = jnp.concatenate([grad_query, grad_keys, grad_values], axis=-1).astype(jnp.bfloat16)
    grad_normed1 = transposed_product(grad_proj, qkv_weight)
    wide_in = stream.astype(jnp.float32)
    normal_one, inv_one = norm_parts(wide_in)
    normed1 = (normal_one * norm1_gain + norm1_bias).astype(jnp.bfloat16)
    normed2 = (normal_two * norm2_gain + norm2_bias).astype(jnp.bfloat16)
    grad_stream = grad_middle + norm_back(grad_normed1 * norm1_gain, normal_one, inv_one)
    both_axes = (0, 1)
    scale_factors = (
        (normed1, grad_proj),
        (context, grad_middle_half),
        (normed2, grad_pre_half),
        (activated, masked_half),
    )
    vector_sums = (
        jnp.sum(grad_normed1 * normal_one, axis=both_axes),
        jnp.sum(grad_normed1, axis=both_axes),
        jnp.concatenate(
            [jnp.sum(grad_query, axis=both_axes), jnp.sum(grad_values, axis=both_axes)]
        ),
        jnp.sum(grad_middle, axis=both_axes),
        jnp.sum(grad_normed2 * normal_two, axis=both_axes),
        jnp.sum(grad_normed2, axis=both_axes),
        jnp.sum(grad_pre, axis=both_axes),
        jnp.sum(masked, axis=both_axes),
    )
    return (grad_stream, scale_factors, vector_sums)


def on_device(
    inputs,
    cotangent,
    live_slots,
    norm1_gain,
    norm1_bias,
    qkv_weight,
    qv_bias,
    out_weight,
    out_bias,
    norm2_gain,
    norm2_bias,
    fc1_weight,
    fc1_bias,
    fc2_weight,
    fc2_bias,
):
    is_first = lax.axis_index("section") == 0
    micro_count, slot_count, length, model_width = inputs.shape
    flat_shape = (micro_count * slot_count, length, model_width)
    small_shards = [
        norm1_gain[0], norm1_bias[0], qv_bias[0], out_bias[0],
        norm2_gain[0], norm2_bias[0], fc1_bias[0], fc2_bias[0],
    ]
    rows = qkv_weight.shape[1]
    small_sizes = [shard.shape[0] for shard in small_shards]
    per_row = sum(small_sizes) // rows
    small_pad = -per_row % LANES
    packed_small = jnp.pad(
        jnp.concatenate(small_shards).reshape(rows, per_row), ((0, 0), (0, small_pad))
    )
    qkv_width = qkv_weight.shape[2]
    head_width = qkv_width + out_weight.shape[2]
    attn_shard = jnp.concatenate([qkv_weight[0], out_weight[0], packed_small], axis=1)
    attn_all = lax.all_gather(attn_shard, "dp", axis=0, tiled=True)
    full_fc1 = lax.all_gather(fc1_weight[0], "dp", axis=0, tiled=True)
    full_fc2 = lax.all_gather(fc2_weight[0], "dp", axis=0, tiled=True)
    small_all = attn_all[:, head_width : head_width + per_row].reshape(-1, sum(small_sizes))
    small_full, begin = [], 0
    for size in small_sizes:
        small_full.append(small_all[:, begin : begin + size].reshape(-1))
        begin += size
    params = (
        small_full[0], small_full[1], attn_all[:, :qkv_width], small_full[2],
        attn_all[:, qkv_width:head_width], small_full[3], small_full[4], small_full[5],
        full_fc1, small_full[6], full_fc2, small_full[7],
    )
    live_scale = live_slots.reshape(-1).astype(jnp.float32)[:, None, None]
    flat_inputs = inputs.reshape(flat_shape)
    early_result, _ = layer_forward(flat_inputs, live_scale, params)
    received = passed_along(early_result, "section", 1)
    stream = jnp.where(is_first, flat_inputs, received)
    result, saved_inputs = layer_forward(stream, live_scale, params)
    top_grad = cotangent.reshape(flat_shape)
    early_back, _, _ = layer_backward(
        top_grad.astype(jnp.float32), live_scale, saved_inputs, params
    )
    received_grad = passed_along(early_back.astype(jnp.bfloat16), "section", -1)
    own_grad = jnp.where(is_first, received_grad, top_grad).astype(jnp.float32)
    grad_stream, factors, sums = layer_backward(own_grad, live_scale, saved_inputs, params)

    def outer_sum(position):
        left_rows, right_rows = factors[position]
        return jnp.einsum(
            "bsd,bse->de", left_rows, right_rows, preferred_element_type=jnp.float32
        ).astype(jnp.bfloat16)

    def scattered(partial):
        return lax.psum_scatter(partial, "dp", scatter_dimension=0, tiled=True).astype(jnp.float32)

    fc2_grad = scattered(outer_sum(3))
    fc1_grad = scattered(outer_sum(2))
    shares = model_width // rows
    small_sums = jnp.concatenate(
        [total.reshape(shares, size) for total, size in zip(sums, small_sizes)], axis=1
    ).reshape(model_width, per_row)
    small_sums = jnp.pad(small_sums, ((0, 0), (0, small_pad))).astype(jnp.bfloat16)
    attn_grad = scattered(jnp.concatenate([outer_sum(0), outer_sum(1), small_sums], axis=1))
    small_flat = attn_grad[:, head_width : head_width + per_row].reshape(-1)
    small_grads, begin = [], 0
    for size in small_sizes:
        small_grads.append(small_flat[begin : begin + size][None])
        begin += size
    return (
        result.reshape(inputs.shape)[None],
        grad_stream.reshape(inputs.shape)[None],
        small_grads[0],
        small_grads[1],
        attn_grad[None, :, :qkv_width],
        small_grads[2],
        attn_grad[None, :, qkv_width:head_width],
        small_grads[3],
        small_grads[4],
        small_grads[5],
        fc1_grad[None],
        small_grads[6],
        fc2_grad[None],
        small_grads[7],
    )


def solution(mesh):
    in_specs = (
        P(None, "dp", None, None),
        P(None, "dp", None, None),
        P(None, "dp"),
        P("section", "dp"),
        P("section", "dp"),
        P("section", "dp", None),
        P("section", "dp"),
        P("section", "dp", None),
        P("section", "dp"),
        P("section", "dp"),
        P("section", "dp"),
        P("section", "dp", None),
        P("section", "dp"),
        P("section", "dp", None),
        P("section", "dp"),
    )
    out_specs = (
        P("section", None, "dp", None, None),
        P("section", None, "dp", None, None),
        P("section", "dp"),
        P("section", "dp"),
        P("section", "dp", None),
        P("section", "dp"),
        P("section", "dp", None),
        P("section", "dp"),
        P("section", "dp"),
        P("section", "dp"),
        P("section", "dp", None),
        P("section", "dp"),
        P("section", "dp", None),
        P("section", "dp"),
    )
    return jax.shard_map(
        on_device, mesh=mesh, in_specs=in_specs, out_specs=out_specs, check_vma=False
    )
```

```python
import jax
import jax.numpy as jnp
from jax import lax
from jax.sharding import PartitionSpec as P

HEAD_DIM = 64
LANES = 128


EPSILON = 1e-06
ROOT_HALF = 0.7071067811865476
INV_ROOT_TWO_PI = 0.3989422804014327


def passed_along(value, axis, steps):
    count = lax.axis_size(axis)
    leading, last = (max(0, -steps), min(count, count - steps))
    return lax.ppermute(value, axis, [(source, source + steps) for source in range(leading, last)])


def norm_parts(stream):
    average = jnp.mean(stream, axis=-1, keepdims=True)
    centred = stream - average
    inv_std = lax.rsqrt(jnp.mean(centred * centred, axis=-1, keepdims=True) + EPSILON)
    return (centred * inv_std, inv_std)


def norm_back(signal, normed, inv_std):
    first_mean = jnp.mean(signal, axis=-1, keepdims=True)
    second_mean = jnp.mean(signal * normed, axis=-1, keepdims=True)
    return inv_std * (signal - first_mean - normed * second_mean)


def gelu_value(pre_act):
    return 0.5 * pre_act * (1.0 + lax.erf(pre_act * ROOT_HALF))


def gelu_slope(pre_act):
    return (
        0.5 * (1.0 + lax.erf(pre_act * ROOT_HALF))
        + pre_act * jnp.exp(-0.5 * pre_act * pre_act) * INV_ROOT_TWO_PI
    )


def matmul(left_rows, weight):
    return jnp.einsum("bsd,de->bse", left_rows, weight, preferred_element_type=jnp.float32)


def transposed_product(left_rows, weight):
    return jnp.einsum("bse,de->bsd", left_rows, weight, preferred_element_type=jnp.float32)


def layer_forward(stream, live_scale, params):
    (
        norm1_gain,
        norm1_bias,
        qkv_weight,
        qv_bias,
        out_weight,
        out_bias,
        norm2_gain,
        norm2_bias,
        fc1_weight,
        fc1_bias,
        fc2_weight,
        fc2_bias,
    ) = params
    images, length, model_width = stream.shape
    heads_shape = (images, length, model_width // HEAD_DIM, HEAD_DIM)
    scaling = HEAD_DIM ** (-0.5)
    wide_in = stream.astype(jnp.float32)
    normal_one, inv_one = norm_parts(wide_in)
    normed1 = (normal_one * norm1_gain + norm1_bias).astype(jnp.bfloat16)
    projected = matmul(normed1, qkv_weight)
    query_rows = (projected[..., :model_width] + qv_bias[:model_width]).astype(jnp.bfloat16)
    key_rows = projected[..., model_width : 2 * model_width].astype(jnp.bfloat16)
    value_rows = (projected[..., 2 * model_width :] + qv_bias[model_width:]).astype(jnp.bfloat16)
    scores = (
        jnp.einsum(
            "bqhe,bkhe->bhqk",
            query_rows.reshape(heads_shape),
            key_rows.reshape(heads_shape),
            preferred_element_type=jnp.float32,
        )
        * scaling
    )
    top_score = jnp.max(scores, axis=-1, keepdims=True)
    exp_scores = jnp.exp(scores - top_score)
    totals = jnp.sum(exp_scores, axis=-1, keepdims=True)
    log_total = top_score + jnp.log(totals)
    attn_probs = (exp_scores / totals).astype(jnp.bfloat16)
    context = jnp.einsum(
        "bhqk,bkhe->bqhe",
        attn_probs,
        value_rows.reshape(heads_shape),
        preferred_element_type=jnp.float32,
    )
    context = context.reshape(images, length, model_width).astype(jnp.bfloat16)
    middle = wide_in + matmul(context, out_weight) + out_bias
    normal_two, inv_two = norm_parts(middle)
    normed2 = (normal_two * norm2_gain + norm2_bias).astype(jnp.bfloat16)
    pre_act = matmul(normed2, fc1_weight) + fc1_bias
    activated = gelu_value(pre_act).astype(jnp.bfloat16)
    result = live_scale * (middle + matmul(activated, fc2_weight) + fc2_bias)
    saved_inputs = (
        stream,
        query_rows,
        key_rows,
        value_rows,
        log_total,
        context,
        middle,
        pre_act,
        activated,
    )
    return (result.astype(jnp.bfloat16), saved_inputs)


def layer_backward(grad_out, live_scale, saved_inputs, params):
    (
        norm1_gain,
        norm1_bias,
        qkv_weight,
        qv_bias,
        out_weight,
        out_bias,
        norm2_gain,
        norm2_bias,
        fc1_weight,
        fc1_bias,
        fc2_weight,
        fc2_bias,
    ) = params
    stream, query_rows, key_rows, value_rows, log_total, context, middle, pre_act, activated = (
        saved_inputs
    )
    images, length, model_width = stream.shape
    heads_shape = (images, length, model_width // HEAD_DIM, HEAD_DIM)
    scaling = HEAD_DIM ** (-0.5)
    masked = live_scale * grad_out
    masked_half = masked.astype(jnp.bfloat16)
    grad_pre = transposed_product(masked_half, fc2_weight) * gelu_slope(pre_act)
    grad_pre_half = grad_pre.astype(jnp.bfloat16)
    grad_normed2 = transposed_product(grad_pre_half, fc1_weight)
    normal_two, inv_two = norm_parts(middle)
    grad_middle = masked + norm_back(grad_normed2 * norm2_gain, normal_two, inv_two)
    grad_middle_half = grad_middle.astype(jnp.bfloat16)
    grad_context = (
        transposed_product(grad_middle_half, out_weight).astype(jnp.bfloat16).reshape(heads_shape)
    )
    query_heads = query_rows.reshape(heads_shape)
    key_heads = key_rows.reshape(heads_shape)
    value_heads = value_rows.reshape(heads_shape)
    scores = (
        jnp.einsum("bqhe,bkhe->bhqk", query_heads, key_heads, preferred_element_type=jnp.float32)
        * scaling
    )
    probs_wide = jnp.exp(scores - log_total)
    probs_half = probs_wide.astype(jnp.bfloat16)
    grad_probs = jnp.einsum(
        "bqhe,bkhe->bhqk", grad_context, value_heads, preferred_element_type=jnp.float32
    )
    row_delta = jnp.sum(probs_wide * grad_probs, axis=-1, keepdims=True)
    grad_scores = (probs_wide * (grad_probs - row_delta) * scaling).astype(jnp.bfloat16)
    grad_query = jnp.einsum(
        "bhqk,bkhe->bqhe", grad_scores, key_heads, preferred_element_type=jnp.float32
    ).reshape(images, length, model_width)
    grad_keys = jnp.einsum(
        "bhqk,bqhe->bkhe", grad_scores, query_heads, preferred_element_type=jnp.float32
    ).reshape(images, length, model_width)
    grad_values = jnp.einsum(
        "bhqk,bqhe->bkhe", probs_half, grad_context, preferred_element_type=jnp.float32
    ).reshape(images, length, model_width)
    grad_proj = jnp.concatenate([grad_query, grad_keys, grad_values], axis=-1).astype(jnp.bfloat16)
    grad_normed1 = transposed_product(grad_proj, qkv_weight)
    wide_in = stream.astype(jnp.float32)
    normal_one, inv_one = norm_parts(wide_in)
    normed1 = (normal_one * norm1_gain + norm1_bias).astype(jnp.bfloat16)
    normed2 = (normal_two * norm2_gain + norm2_bias).astype(jnp.bfloat16)
    grad_stream = grad_middle + norm_back(grad_normed1 * norm1_gain, normal_one, inv_one)
    both_axes = (0, 1)
    scale_factors = (
        (normed1, grad_proj),
        (context, grad_middle_half),
        (normed2, grad_pre_half),
        (activated, masked_half),
    )
    vector_sums = (
        jnp.sum(grad_normed1 * normal_one, axis=both_axes),
        jnp.sum(grad_normed1, axis=both_axes),
        jnp.concatenate(
            [jnp.sum(grad_query, axis=both_axes), jnp.sum(grad_values, axis=both_axes)]
        ),
        jnp.sum(grad_middle, axis=both_axes),
        jnp.sum(grad_normed2 * normal_two, axis=both_axes),
        jnp.sum(grad_normed2, axis=both_axes),
        jnp.sum(grad_pre, axis=both_axes),
        jnp.sum(masked, axis=both_axes),
    )
    return (grad_stream, scale_factors, vector_sums)


GRID_DEPTH = 4
GRID_SIZE = 16


def swapped(value, offset):
    return lax.ppermute(value, "dp", [(i, i ^ offset) for i in range(GRID_SIZE)])


def added(left, right):
    return (left.astype(jnp.float32) + right.astype(jnp.float32)).astype(jnp.bfloat16)


def picked(value, index, axis):
    return lax.dynamic_index_in_dim(value, index, axis, keepdims=False)


def pair_sum(value, own, offset, axis):
    arrived = swapped(picked(value, 1 - own, axis), offset)
    return added(picked(value, own, axis), arrived)


def line_sum(value, depth):
    stride = GRID_SIZE // GRID_DEPTH
    last = GRID_DEPTH - 1
    up = down = None
    for step in range(last):
        up_part = picked(value, jnp.minimum(depth + last - step, last), 0)
        down_part = picked(value, jnp.maximum(depth - last + step, 0), 0)
        if step:
            up_part, down_part = added(up_part, up), added(down_part, down)
        pairs = [(i, i + stride) for i in range((step + 1) * stride)]
        up = lax.ppermute(up_part, "dp", pairs)
        down = lax.ppermute(
            down_part, "dp", [(GRID_SIZE - 1 - a, GRID_SIZE - 1 - b) for a, b in pairs]
        )
    return picked(value, depth, 0).astype(jnp.float32) + up + down


def grid_scatter(partial, side_first):
    me = lax.axis_index("dp")
    depth, side, core = me // 4, me // 2 % 2, me % 2
    rows, width = partial.shape
    share = rows // GRID_SIZE
    parts = partial.reshape(2 * GRID_DEPTH, 2, share, width)
    parts = pair_sum(parts, core, 1, 1).reshape(GRID_DEPTH, 2, share, width)
    if side_first:
        return line_sum(pair_sum(parts, side, 2, 1), depth)
    both = line_sum(parts, depth).astype(jnp.bfloat16)
    arrived = swapped(picked(both, 1 - side, 0), 2)
    return picked(both, side, 0).astype(jnp.float32) + arrived


def on_device(
    inputs,
    cotangent,
    live_slots,
    norm1_gain,
    norm1_bias,
    qkv_weight,
    qv_bias,
    out_weight,
    out_bias,
    norm2_gain,
    norm2_bias,
    fc1_weight,
    fc1_bias,
    fc2_weight,
    fc2_bias,
):
    is_first = lax.axis_index("section") == 0
    micro_count, slot_count, length, model_width = inputs.shape
    flat_shape = (micro_count * slot_count, length, model_width)
    small_shards = [
        norm1_gain[0], norm1_bias[0], qv_bias[0], out_bias[0],
        norm2_gain[0], norm2_bias[0], fc1_bias[0], fc2_bias[0],
    ]
    rows = qkv_weight.shape[1]
    small_sizes = [shard.shape[0] for shard in small_shards]
    per_row = sum(small_sizes) // rows
    small_pad = -per_row % LANES
    packed_small = jnp.pad(
        jnp.concatenate(small_shards).reshape(rows, per_row), ((0, 0), (0, small_pad))
    )
    qkv_width = qkv_weight.shape[2]
    head_width = qkv_width + out_weight.shape[2]
    attn_shard = jnp.concatenate([qkv_weight[0], out_weight[0], packed_small], axis=1)
    attn_all = lax.all_gather(attn_shard, "dp", axis=0, tiled=True)
    full_fc1 = lax.all_gather(fc1_weight[0], "dp", axis=0, tiled=True)
    full_fc2 = lax.all_gather(fc2_weight[0], "dp", axis=0, tiled=True)
    small_all = attn_all[:, head_width : head_width + per_row].reshape(-1, sum(small_sizes))
    small_full, begin = [], 0
    for size in small_sizes:
        small_full.append(small_all[:, begin : begin + size].reshape(-1))
        begin += size
    params = (
        small_full[0], small_full[1], attn_all[:, :qkv_width], small_full[2],
        attn_all[:, qkv_width:head_width], small_full[3], small_full[4], small_full[5],
        full_fc1, small_full[6], full_fc2, small_full[7],
    )
    live_scale = live_slots.reshape(-1).astype(jnp.float32)[:, None, None]
    flat_inputs = inputs.reshape(flat_shape)
    early_result, _ = layer_forward(flat_inputs, live_scale, params)
    received = passed_along(early_result, "section", 1)
    stream = jnp.where(is_first, flat_inputs, received)
    result, saved_inputs = layer_forward(stream, live_scale, params)
    top_grad = cotangent.reshape(flat_shape)
    early_back, _, _ = layer_backward(
        top_grad.astype(jnp.float32), live_scale, saved_inputs, params
    )
    received_grad = passed_along(early_back.astype(jnp.bfloat16), "section", -1)
    own_grad = jnp.where(is_first, received_grad, top_grad).astype(jnp.float32)
    grad_stream, factors, sums = layer_backward(own_grad, live_scale, saved_inputs, params)

    def outer_sum(position):
        left_rows, right_rows = factors[position]
        return jnp.einsum(
            "bsd,bse->de", left_rows, right_rows, preferred_element_type=jnp.float32
        ).astype(jnp.bfloat16)

    def scattered(partial, side_first):
        if lax.axis_size("dp") == GRID_SIZE:
            return grid_scatter(partial, side_first)
        return lax.psum_scatter(partial, "dp", scatter_dimension=0, tiled=True).astype(jnp.float32)

    fc2_grad = scattered(outer_sum(3), True)
    fc1_grad = scattered(outer_sum(2), False)
    shares = model_width // rows
    small_sums = jnp.concatenate(
        [total.reshape(shares, size) for total, size in zip(sums, small_sizes)], axis=1
    ).reshape(model_width, per_row)
    small_sums = jnp.pad(small_sums, ((0, 0), (0, small_pad))).astype(jnp.bfloat16)
    out_grad = scattered(outer_sum(1), True)
    qkv_sums = outer_sum(0)
    half = qkv_width // 2
    qkv_left = scattered(qkv_sums[:, :half], True)
    qkv_right = scattered(jnp.concatenate([qkv_sums[:, half:], small_sums], axis=1), False)
    qkv_grad = jnp.concatenate([qkv_left, qkv_right[:, :half]], axis=1)
    small_flat = qkv_right[:, half : half + per_row].reshape(-1)
    small_grads, begin = [], 0
    for size in small_sizes:
        small_grads.append(small_flat[begin : begin + size][None])
        begin += size
    return (
        result.reshape(inputs.shape)[None],
        grad_stream.reshape(inputs.shape)[None],
        small_grads[0],
        small_grads[1],
        qkv_grad[None],
        small_grads[2],
        out_grad[None],
        small_grads[3],
        small_grads[4],
        small_grads[5],
        fc1_grad[None],
        small_grads[6],
        fc2_grad[None],
        small_grads[7],
    )


def solution(mesh):
    in_specs = (
        P(None, "dp", None, None),
        P(None, "dp", None, None),
        P(None, "dp"),
        P("section", "dp"),
        P("section", "dp"),
        P("section", "dp", None),
        P("section", "dp"),
        P("section", "dp", None),
        P("section", "dp"),
        P("section", "dp"),
        P("section", "dp"),
        P("section", "dp", None),
        P("section", "dp"),
        P("section", "dp", None),
        P("section", "dp"),
    )
    out_specs = (
        P("section", None, "dp", None, None),
        P("section", None, "dp", None, None),
        P("section", "dp"),
        P("section", "dp"),
        P("section", "dp", None),
        P("section", "dp"),
        P("section", "dp", None),
        P("section", "dp"),
        P("section", "dp"),
        P("section", "dp"),
        P("section", "dp", None),
        P("section", "dp"),
        P("section", "dp", None),
        P("section", "dp"),
    )
    return jax.shard_map(
        on_device, mesh=mesh, in_specs=in_specs, out_specs=out_specs, check_vma=False
    )
```

```python
import jax
import jax.numpy as jnp
from jax import lax
from jax.sharding import PartitionSpec as P

HEAD_DIM = 64
LANES = 128


EPSILON = 1e-06
ROOT_HALF = 0.7071067811865476
INV_ROOT_TWO_PI = 0.3989422804014327


def passed_along(value, axis, steps):
    count = lax.axis_size(axis)
    leading, last = (max(0, -steps), min(count, count - steps))
    return lax.ppermute(value, axis, [(source, source + steps) for source in range(leading, last)])


def norm_parts(stream):
    average = jnp.mean(stream, axis=-1, keepdims=True)
    centred = stream - average
    inv_std = lax.rsqrt(jnp.mean(centred * centred, axis=-1, keepdims=True) + EPSILON)
    return (centred * inv_std, inv_std)


def norm_back(signal, normed, inv_std):
    first_mean = jnp.mean(signal, axis=-1, keepdims=True)
    second_mean = jnp.mean(signal * normed, axis=-1, keepdims=True)
    return inv_std * (signal - first_mean - normed * second_mean)


def gelu_value(pre_act):
    return 0.5 * pre_act * (1.0 + lax.erf(pre_act * ROOT_HALF))


def gelu_slope(pre_act):
    return (
        0.5 * (1.0 + lax.erf(pre_act * ROOT_HALF))
        + pre_act * jnp.exp(-0.5 * pre_act * pre_act) * INV_ROOT_TWO_PI
    )


def matmul(left_rows, weight):
    return jnp.einsum("bsd,de->bse", left_rows, weight, preferred_element_type=jnp.float32)


def transposed_product(left_rows, weight):
    return jnp.einsum("bse,de->bsd", left_rows, weight, preferred_element_type=jnp.float32)


def layer_forward(stream, live_scale, params):
    (
        norm1_gain,
        norm1_bias,
        qkv_weight,
        qv_bias,
        out_weight,
        out_bias,
        norm2_gain,
        norm2_bias,
        fc1_weight,
        fc1_bias,
        fc2_weight,
        fc2_bias,
    ) = params
    images, length, model_width = stream.shape
    heads_shape = (images, length, model_width // HEAD_DIM, HEAD_DIM)
    scaling = HEAD_DIM ** (-0.5)
    wide_in = stream.astype(jnp.float32)
    normal_one, inv_one = norm_parts(wide_in)
    normed1 = (normal_one * norm1_gain + norm1_bias).astype(jnp.bfloat16)
    projected = matmul(normed1, qkv_weight)
    query_rows = (projected[..., :model_width] + qv_bias[:model_width]).astype(jnp.bfloat16)
    key_rows = projected[..., model_width : 2 * model_width].astype(jnp.bfloat16)
    value_rows = (projected[..., 2 * model_width :] + qv_bias[model_width:]).astype(jnp.bfloat16)
    scores = (
        jnp.einsum(
            "bqhe,bkhe->bhqk",
            query_rows.reshape(heads_shape),
            key_rows.reshape(heads_shape),
            preferred_element_type=jnp.float32,
        )
        * scaling
    )
    top_score = jnp.max(scores, axis=-1, keepdims=True)
    exp_scores = jnp.exp(scores - top_score)
    totals = jnp.sum(exp_scores, axis=-1, keepdims=True)
    log_total = top_score + jnp.log(totals)
    attn_probs = (exp_scores / totals).astype(jnp.bfloat16)
    context = jnp.einsum(
        "bhqk,bkhe->bqhe",
        attn_probs,
        value_rows.reshape(heads_shape),
        preferred_element_type=jnp.float32,
    )
    context = context.reshape(images, length, model_width).astype(jnp.bfloat16)
    middle = wide_in + matmul(context, out_weight) + out_bias
    normal_two, inv_two = norm_parts(middle)
    normed2 = (normal_two * norm2_gain + norm2_bias).astype(jnp.bfloat16)
    pre_act = matmul(normed2, fc1_weight) + fc1_bias
    activated = gelu_value(pre_act).astype(jnp.bfloat16)
    result = live_scale * (middle + matmul(activated, fc2_weight) + fc2_bias)
    saved_inputs = (
        stream,
        query_rows,
        key_rows,
        value_rows,
        log_total,
        context,
        middle,
        pre_act,
        activated,
    )
    return (result.astype(jnp.bfloat16), saved_inputs)


def layer_backward(grad_out, live_scale, saved_inputs, params, send_early=False):
    (
        norm1_gain,
        norm1_bias,
        qkv_weight,
        qv_bias,
        out_weight,
        out_bias,
        norm2_gain,
        norm2_bias,
        fc1_weight,
        fc1_bias,
        fc2_weight,
        fc2_bias,
    ) = params
    stream, query_rows, key_rows, value_rows, log_total, context, middle, pre_act, activated = (
        saved_inputs
    )
    images, length, model_width = stream.shape
    heads_shape = (images, length, model_width // HEAD_DIM, HEAD_DIM)
    scaling = HEAD_DIM ** (-0.5)
    masked = live_scale * grad_out
    masked_half = masked.astype(jnp.bfloat16)
    early_sums = ()
    if send_early:
        fc2_sums = outer_sum(activated, masked_half)
        masked_half, fc2_sums = lax.optimization_barrier((masked_half, fc2_sums))
        fc2_parts = core_stage(fc2_sums)
    grad_pre = transposed_product(masked_half, fc2_weight) * gelu_slope(pre_act)
    grad_pre_half = grad_pre.astype(jnp.bfloat16)
    grad_normed2 = transposed_product(grad_pre_half, fc1_weight)
    normal_two, inv_two = norm_parts(middle)
    grad_middle = masked + norm_back(grad_normed2 * norm2_gain, normal_two, inv_two)
    grad_middle_half = grad_middle.astype(jnp.bfloat16)
    if send_early:
        normed2 = (normal_two * norm2_gain + norm2_bias).astype(jnp.bfloat16)
        fc1_sums = outer_sum(normed2, grad_pre_half)
        grad_middle_half, fc1_sums, fc2_parts = lax.optimization_barrier(
            (grad_middle_half, fc1_sums, fc2_parts)
        )
        fc1_parts = core_stage(fc1_sums)
    grad_context = (
        transposed_product(grad_middle_half, out_weight).astype(jnp.bfloat16).reshape(heads_shape)
    )
    query_heads = query_rows.reshape(heads_shape)
    key_heads = key_rows.reshape(heads_shape)
    value_heads = value_rows.reshape(heads_shape)
    scores = (
        jnp.einsum("bqhe,bkhe->bhqk", query_heads, key_heads, preferred_element_type=jnp.float32)
        * scaling
    )
    probs_wide = jnp.exp(scores - log_total)
    probs_half = probs_wide.astype(jnp.bfloat16)
    grad_probs = jnp.einsum(
        "bqhe,bkhe->bhqk", grad_context, value_heads, preferred_element_type=jnp.float32
    )
    row_delta = jnp.sum(probs_wide * grad_probs, axis=-1, keepdims=True)
    grad_scores = (probs_wide * (grad_probs - row_delta) * scaling).astype(jnp.bfloat16)
    if send_early:
        out_sums = outer_sum(context, grad_middle_half)
        grad_scores, out_sums, fc1_parts = lax.optimization_barrier(
            (grad_scores, out_sums, fc1_parts)
        )
        early_sums = (fc2_parts, fc1_parts, core_stage(out_sums))
    grad_query = jnp.einsum(
        "bhqk,bkhe->bqhe", grad_scores, key_heads, preferred_element_type=jnp.float32
    ).reshape(images, length, model_width)
    grad_keys = jnp.einsum(
        "bhqk,bqhe->bkhe", grad_scores, query_heads, preferred_element_type=jnp.float32
    ).reshape(images, length, model_width)
    grad_values = jnp.einsum(
        "bhqk,bqhe->bkhe", probs_half, grad_context, preferred_element_type=jnp.float32
    ).reshape(images, length, model_width)
    grad_proj = jnp.concatenate([grad_query, grad_keys, grad_values], axis=-1).astype(jnp.bfloat16)
    grad_normed1 = transposed_product(grad_proj, qkv_weight)
    wide_in = stream.astype(jnp.float32)
    normal_one, inv_one = norm_parts(wide_in)
    normed1 = (normal_one * norm1_gain + norm1_bias).astype(jnp.bfloat16)
    normed2 = (normal_two * norm2_gain + norm2_bias).astype(jnp.bfloat16)
    grad_stream = grad_middle + norm_back(grad_normed1 * norm1_gain, normal_one, inv_one)
    both_axes = (0, 1)
    scale_factors = (
        (normed1, grad_proj),
        (context, grad_middle_half),
        (normed2, grad_pre_half),
        (activated, masked_half),
    )
    vector_sums = (
        jnp.sum(grad_normed1 * normal_one, axis=both_axes),
        jnp.sum(grad_normed1, axis=both_axes),
        jnp.concatenate(
            [jnp.sum(grad_query, axis=both_axes), jnp.sum(grad_values, axis=both_axes)]
        ),
        jnp.sum(grad_middle, axis=both_axes),
        jnp.sum(grad_normed2 * normal_two, axis=both_axes),
        jnp.sum(grad_normed2, axis=both_axes),
        jnp.sum(grad_pre, axis=both_axes),
        jnp.sum(masked, axis=both_axes),
    )
    return (grad_stream, scale_factors, vector_sums, early_sums)


GRID_DEPTH = 4
GRID_SIZE = 16


def swapped(value, offset):
    return lax.ppermute(value, "dp", [(i, i ^ offset) for i in range(GRID_SIZE)])


def added(left, right):
    return (left.astype(jnp.float32) + right.astype(jnp.float32)).astype(jnp.bfloat16)


def picked(value, index, axis):
    return lax.dynamic_index_in_dim(value, index, axis, keepdims=False)


def pair_sum(value, own, offset, axis):
    arrived = swapped(picked(value, 1 - own, axis), offset)
    return added(picked(value, own, axis), arrived)


def line_sum(value, depth):
    stride = GRID_SIZE // GRID_DEPTH
    last = GRID_DEPTH - 1
    up = down = None
    for step in range(last):
        up_part = picked(value, jnp.minimum(depth + last - step, last), 0)
        down_part = picked(value, jnp.maximum(depth - last + step, 0), 0)
        if step:
            up_part, down_part = added(up_part, up), added(down_part, down)
        pairs = [(i, i + stride) for i in range((step + 1) * stride)]
        up = lax.ppermute(up_part, "dp", pairs)
        down = lax.ppermute(
            down_part, "dp", [(GRID_SIZE - 1 - a, GRID_SIZE - 1 - b) for a, b in pairs]
        )
    return picked(value, depth, 0).astype(jnp.float32) + up + down


def core_stage(partial):
    if lax.axis_size("dp") != GRID_SIZE:
        return partial
    rows, width = partial.shape
    parts = partial.reshape(2 * GRID_DEPTH, 2, rows // GRID_SIZE, width)
    parts = pair_sum(parts, lax.axis_index("dp") % 2, 1, 1)
    return parts.reshape(GRID_DEPTH, 2, rows // GRID_SIZE, width)


def scattered(parts, side_first):
    if lax.axis_size("dp") != GRID_SIZE:
        return lax.psum_scatter(parts, "dp", scatter_dimension=0, tiled=True).astype(jnp.float32)
    me = lax.axis_index("dp")
    depth, side = me // 4, me // 2 % 2
    if side_first:
        return line_sum(pair_sum(parts, side, 2, 1), depth)
    both = line_sum(parts, depth).astype(jnp.bfloat16)
    arrived = swapped(picked(both, 1 - side, 0), 2)
    return picked(both, side, 0).astype(jnp.float32) + arrived


def outer_sum(left_rows, right_rows):
    return jnp.einsum(
        "bsd,bse->de", left_rows, right_rows, preferred_element_type=jnp.float32
    ).astype(jnp.bfloat16)


def on_device(
    inputs,
    cotangent,
    live_slots,
    norm1_gain,
    norm1_bias,
    qkv_weight,
    qv_bias,
    out_weight,
    out_bias,
    norm2_gain,
    norm2_bias,
    fc1_weight,
    fc1_bias,
    fc2_weight,
    fc2_bias,
):
    is_first = lax.axis_index("section") == 0
    micro_count, slot_count, length, model_width = inputs.shape
    flat_shape = (micro_count * slot_count, length, model_width)
    small_shards = [
        norm1_gain[0], norm1_bias[0], qv_bias[0], out_bias[0],
        norm2_gain[0], norm2_bias[0], fc1_bias[0], fc2_bias[0],
    ]
    rows = qkv_weight.shape[1]
    small_sizes = [shard.shape[0] for shard in small_shards]
    per_row = sum(small_sizes) // rows
    small_pad = -per_row % LANES
    packed_small = jnp.pad(
        jnp.concatenate(small_shards).reshape(rows, per_row), ((0, 0), (0, small_pad))
    )
    qkv_width = qkv_weight.shape[2]
    head_width = qkv_width + out_weight.shape[2]
    attn_shard = jnp.concatenate([qkv_weight[0], out_weight[0], packed_small], axis=1)
    attn_all = lax.all_gather(attn_shard, "dp", axis=0, tiled=True)
    full_fc1 = lax.all_gather(fc1_weight[0], "dp", axis=0, tiled=True)
    full_fc2 = lax.all_gather(fc2_weight[0], "dp", axis=0, tiled=True)
    small_all = attn_all[:, head_width : head_width + per_row].reshape(-1, sum(small_sizes))
    small_full, begin = [], 0
    for size in small_sizes:
        small_full.append(small_all[:, begin : begin + size].reshape(-1))
        begin += size
    params = (
        small_full[0], small_full[1], attn_all[:, :qkv_width], small_full[2],
        attn_all[:, qkv_width:head_width], small_full[3], small_full[4], small_full[5],
        full_fc1, small_full[6], full_fc2, small_full[7],
    )
    live_scale = live_slots.reshape(-1).astype(jnp.float32)[:, None, None]
    flat_inputs = inputs.reshape(flat_shape)
    early_result, _ = layer_forward(flat_inputs, live_scale, params)
    received = passed_along(early_result, "section", 1)
    stream = jnp.where(is_first, flat_inputs, received)
    result, saved_inputs = layer_forward(stream, live_scale, params)
    top_grad = cotangent.reshape(flat_shape)
    early_back, _, _, _ = layer_backward(
        top_grad.astype(jnp.float32), live_scale, saved_inputs, params
    )
    received_grad = passed_along(early_back.astype(jnp.bfloat16), "section", -1)
    own_grad = jnp.where(is_first, received_grad, top_grad).astype(jnp.float32)
    grad_stream, factors, sums, early_sums = layer_backward(
        own_grad, live_scale, saved_inputs, params, send_early=True
    )

    fc2_grad = scattered(early_sums[0], True)
    fc1_grad = scattered(early_sums[1], False)
    shares = model_width // rows
    small_sums = jnp.concatenate(
        [total.reshape(shares, size) for total, size in zip(sums, small_sizes)], axis=1
    ).reshape(model_width, per_row)
    small_sums = jnp.pad(small_sums, ((0, 0), (0, small_pad))).astype(jnp.bfloat16)
    out_grad = scattered(early_sums[2], True)
    qkv_sums = outer_sum(*factors[0])
    half = qkv_width // 2
    qkv_left = scattered(core_stage(qkv_sums[:, :half]), True)
    qkv_right = scattered(
        core_stage(jnp.concatenate([qkv_sums[:, half:], small_sums], axis=1)), False
    )
    qkv_grad = jnp.concatenate([qkv_left, qkv_right[:, :half]], axis=1)
    small_flat = qkv_right[:, half : half + per_row].reshape(-1)
    small_grads, begin = [], 0
    for size in small_sizes:
        small_grads.append(small_flat[begin : begin + size][None])
        begin += size
    return (
        result.reshape(inputs.shape)[None],
        grad_stream.reshape(inputs.shape)[None],
        small_grads[0],
        small_grads[1],
        qkv_grad[None],
        small_grads[2],
        out_grad[None],
        small_grads[3],
        small_grads[4],
        small_grads[5],
        fc1_grad[None],
        small_grads[6],
        fc2_grad[None],
        small_grads[7],
    )


def solution(mesh):
    in_specs = (
        P(None, "dp", None, None),
        P(None, "dp", None, None),
        P(None, "dp"),
        P("section", "dp"),
        P("section", "dp"),
        P("section", "dp", None),
        P("section", "dp"),
        P("section", "dp", None),
        P("section", "dp"),
        P("section", "dp"),
        P("section", "dp"),
        P("section", "dp", None),
        P("section", "dp"),
        P("section", "dp", None),
        P("section", "dp"),
    )
    out_specs = (
        P("section", None, "dp", None, None),
        P("section", None, "dp", None, None),
        P("section", "dp"),
        P("section", "dp"),
        P("section", "dp", None),
        P("section", "dp"),
        P("section", "dp", None),
        P("section", "dp"),
        P("section", "dp"),
        P("section", "dp"),
        P("section", "dp", None),
        P("section", "dp"),
        P("section", "dp", None),
        P("section", "dp"),
    )
    return jax.shard_map(
        on_device, mesh=mesh, in_specs=in_specs, out_specs=out_specs, check_vma=False
    )
```
